32 devices in a mesh: expert: 8 (over y, x, core), dp: 4 (over z).
Axes of the slice: x: 2, y: 2, z: 4, core: 2. Of those that a mesh axis runs over, the one named last changes fastest.
Arguments:
- tokens: bfloat16 [4096, 1024], P(('expert', 'dp')), may hold values from -6 to 6
- expert_ids: int32 [4096, 8], P(('expert', 'dp')), may hold values from 0 to 15, all different within a row; in each aligned block of 128 rows (0 to 127, 128 to 255, ...) at most 96 rows name the same one
- combine_weights: float32 [4096, 8], P(('expert', 'dp')), may hold values from 0.2 to 1
- lift_weights: bfloat16 [16, 1024, 768], P('expert', 'dp'), may hold values from -0.1875 to 0.1875
- down_weights: bfloat16 [16, 384, 1024], P('expert', None, 'dp'), may hold values from -0.3125 to 0.3125
- cotangent: bfloat16 [4096, 1024], P(('expert', 'dp')), may hold values from -1.5 to 1.5
Outputs:
- layer_output: bfloat16 [4096, 1024], P(('expert', 'dp'))
- token_grads: bfloat16 [4096, 1024], P(('expert', 'dp'))
- lift_grads: bfloat16 [16, 1024, 768], P('expert', 'dp')
- down_grads: bfloat16 [16, 384, 1024], P('expert', None, 'dp')
The draws below stay inside these ranges and needn't reach their ends.
Inputs may be any that keep to these rules, and one draw needn't show every extreme that they name: `expert_ids`: each row names 8 different experts. Among the 128 rows of one device, no expert is named more than 96 times, and in every draw some expert is named exactly 96 times in some device's rows.
All inputs are finite; a program needn't handle non-finite values.
Results may differ from the reference program's by a relative error of at most 0.02.
Values may be sent and summed in bfloat16 or wider, within the bound.
A program may use at most 64 MiB of HBM per device.

```python
import math
import jax
import jax.numpy as jnp
import numpy as np
from jax import lax

D = 1024
FF = 384
TOPK = 8
TOK_DEV = 128
EXPERTS = 16
TOKENS = 4096
CAP = 96
N_EXPERT = 8
N_DP = 4


def block_scale(rng, dims, pieces, least, high):
    gain = 1.0
    for dim, blocks in pieces:
        heights = jax.random.uniform(jax.random.fold_in(jax.random.fold_in(rng, 6), dim), (blocks,), jnp.float32, least / len(pieces), high / len(pieces))
        gain = gain * jnp.repeat(jnp.exp(heights), dims[dim] // blocks).reshape((-1,) + (1,) * (len(dims) - 1 - dim))
    return gain


def assign_block(rng, own, number, rows, count, top, most, skew):
    order = jax.random.permutation(rng, count)
    packed, common = shares(count, rows * top, most, skew, True), shares(count, rows * top, most, skew, False)
    places = jnp.arange(count)

    def named(sizes, turn):
        used = int((sizes > 0).sum())
        fixed = max(1, used // 4)
        passed = fixed + (places - fixed + turn * (used - fixed)) % max(1, count - fixed)
        return jnp.zeros((count,), jnp.int32).at[order[jnp.where(places < fixed, places, passed)]].set(jnp.asarray(sizes, jnp.int32))

    sizes = jnp.where(number % 4 == 0, named(packed, number // 4), named(common, number - number // 4 - 1))
    mixed = jax.random.permutation(jax.random.fold_in(own, 3), count)
    donor, sink = mixed[0:count // 2 * 2:2], mixed[1:count // 2 * 2:2]
    margin = jnp.minimum(sizes[donor] - 1, most - sizes[sink]) // 2
    margin = jnp.where((donor == order[0]) | (sink == order[0]) | (sizes[sink] == 0), 0, jnp.maximum(margin, 0))
    passed = jax.random.randint(jax.random.fold_in(own, 4), (count // 2,), 0, 1 << 20) % (margin + 1)
    sizes = sizes.at[donor].add(-passed).at[sink].add(passed)
    members = jnp.searchsorted(jnp.cumsum(sizes), jnp.arange(rows * top), side="right").astype(jnp.int32)
    listing = members.reshape(top, rows).T
    listing = listing[jax.random.permutation(jax.random.fold_in(own, 1), rows)]
    turn = jax.random.randint(jax.random.fold_in(own, 2), (rows, 1), 0, top)
    return jnp.take_along_axis(listing, (jnp.arange(top)[None, :] + turn) % top, axis=1)


def shares(number_of, total, limit, slope, full):
    weights = [(1 << 20) // math.isqrt(rank ** slope) + 1 for rank in range(1, number_of + 1)]
    largest = limit if full else min(limit, max(-(-total // number_of), total * weights[0] // sum(weights)))
    least = 1 if total - largest >= number_of - 1 else 0
    holding, spare = [largest] + [least] * (number_of - 1), total - largest - least * (number_of - 1)
    while spare > 0:
        movable = [i for i in range(1, number_of) if holding[i] < largest] or [i for i in range(1, number_of) if holding[i] < limit]
        whole, remaining = sum([weights[i] for i in movable]), spare
        for i in movable:
            addition = min(limit - holding[i], max(1, remaining * weights[i] // whole), spare)
            holding[i] = holding[i] + addition
            spare = spare - addition
    return np.array(holding)


def scatter_about(rng, shape, spread, bound, split=(), kind=jnp.bfloat16):
    entries = jax.random.normal(rng, shape, jnp.float32) * spread
    if len(split) > 0:
        entries = block_scale(rng, shape, split, -0.22, 0.18) * entries
    return jnp.clip(entries, min=-bound, max=bound).astype(kind)


def setup_inputs(seed: int = 0) -> dict:
    key_list = jax.random.split(jax.random.key(seed), 7)
    tokens = scatter_about(key_list[0], (TOKENS, D), 1.0, 6.0, ((0, 32),))
    expert_ids_keys = jax.random.split(jax.random.fold_in(key_list[1], 1), TOKENS // TOK_DEV)
    expert_ids_turns = jax.random.permutation(jax.random.fold_in(key_list[1], 3), TOKENS // TOK_DEV)
    expert_ids = jax.vmap(lambda own, number: assign_block(jax.random.fold_in(key_list[1], 2), own, number, TOK_DEV, EXPERTS, TOPK, CAP, 2))(expert_ids_keys, expert_ids_turns).reshape((TOKENS, TOPK))
    combine_weights = jnp.clip(0.2 + 0.8 * jax.random.uniform(key_list[2], (TOKENS, TOPK), jnp.float32) ** block_scale(key_list[2], (TOKENS, TOPK), ((0, 32),), -0.2, 0.2), 0.2, 1.0)
    lift_weights = scatter_about(key_list[3], (EXPERTS, D, 2 * FF), D ** -0.5, 0.1875, ((0, 8), (1, 4)))
    down_weights = scatter_about(key_list[4], (EXPERTS, FF, D), FF ** -0.5, 0.3125, ((0, 8), (2, 4)))
    cotangent = scatter_about(key_list[5], (TOKENS, D), 0.25, 1.5, ((0, 32),))
    return {"tokens": tokens, "expert_ids": expert_ids, "combine_weights": combine_weights, "lift_weights": lift_weights, "down_weights": down_weights, "cotangent": cotangent}


def swish_parts(gate_part):
    sigmoid_val = jax.nn.sigmoid(gate_part)
    return gate_part * sigmoid_val, sigmoid_val * (1.0 + gate_part * (1.0 - sigmoid_val))


def rounded_sum(total, term):
    narrow = lax.optimization_barrier(term.astype(jnp.bfloat16))
    return total + narrow.astype(jnp.float32)


def reference(tokens, expert_ids, combine_weights, lift_weights, down_weights, cotangent):
    capacity_rows = N_EXPERT * CAP
    token_group = (jnp.arange(TOKENS, dtype=jnp.int32) // TOK_DEV) % N_DP
    group_keys = (expert_ids * N_DP + token_group[:, None]).reshape(-1).astype(jnp.int32)
    ordering = jnp.argsort(group_keys, stable=True).astype(jnp.int32)
    counted = jnp.zeros((EXPERTS * N_DP,), jnp.int32).at[group_keys].add(1)
    starting = (jnp.cumsum(counted) - counted).astype(jnp.int32)
    ordering = jnp.concatenate([ordering, jnp.zeros((capacity_rows,), jnp.int32)])
    flat_weights = combine_weights.reshape(-1)
    positions = jnp.arange(capacity_rows, dtype=jnp.int32)

    def per_expert(running, expert):
        out_sum, grad_sum = running
        lift_matrix = lift_weights[expert]
        down_matrix = down_weights[expert]
        lift_total = jnp.zeros((D, 2 * FF), jnp.float32)
        down_total = jnp.zeros((FF, D), jnp.float32)
        for group_index in range(N_DP):
            pair_key = expert * N_DP + group_index
            picked = lax.dynamic_slice(ordering, (starting[pair_key],), (capacity_rows,))
            is_valid = positions < counted[pair_key]
            row_ids = picked // TOPK
            weight_vals = jnp.where(is_valid, flat_weights[picked], jnp.zeros((), flat_weights.dtype))
            inputs = jnp.where(is_valid[:, None], tokens[row_ids], jnp.zeros((), tokens.dtype))
            back_in = (weight_vals[:, None] * cotangent[row_ids].astype(jnp.float32)).astype(jnp.bfloat16)
            hidden = jnp.dot(inputs, lift_matrix, preferred_element_type=jnp.float32)
            gate_part = hidden[:, :FF]
            up_part = hidden[:, FF:]
            swished, slopes = swish_parts(gate_part)
            activated = (swished * up_part).astype(jnp.bfloat16)
            result = jnp.dot(activated, down_matrix, preferred_element_type=jnp.float32).astype(jnp.bfloat16)
            out_sum = out_sum.at[row_ids].add(weight_vals[:, None] * result.astype(jnp.float32))
            grad_act = jnp.dot(back_in, down_matrix.T, preferred_element_type=jnp.float32)
            grad_hidden = jnp.concatenate([grad_act * up_part * slopes, grad_act * swished], axis=1).astype(jnp.bfloat16)
            grad_rows = jnp.dot(grad_hidden, lift_matrix.T, preferred_element_type=jnp.float32).astype(jnp.bfloat16)
            grad_sum = grad_sum.at[row_ids].add(jnp.where(is_valid[:, None], grad_rows.astype(jnp.float32), jnp.zeros((), jnp.float32)))
            lift_total = rounded_sum(lift_total, jnp.dot(inputs.T, grad_hidden, preferred_element_type=jnp.float32))
            down_total = rounded_sum(down_total, jnp.dot(activated.T, back_in, preferred_element_type=jnp.float32))
        return (out_sum, grad_sum), (lift_total.astype(jnp.bfloat16), down_total.astype(jnp.bfloat16))

    start_sums = (jnp.zeros((TOKENS, D), jnp.float32), jnp.zeros((TOKENS, D), jnp.float32))
    sums_out, grads_out = lax.scan(per_expert, start_sums, jnp.arange(EXPERTS, dtype=jnp.int32))
    out_sum, grad_sum = sums_out
    lift_grads, down_grads = grads_out
    return out_sum.astype(jnp.bfloat16), grad_sum.astype(jnp.bfloat16), lift_grads, down_grads
```

```python
import jax
import jax.numpy as jnp
from jax import lax
from jax.sharding import PartitionSpec as P


def swish_parts(gate_part):
    sigmoid_val = jax.nn.sigmoid(gate_part)
    return (gate_part * sigmoid_val, sigmoid_val * (1.0 + gate_part * (1.0 - sigmoid_val)))


def collect(returned, target, tok_rows, top_count):
    flat_back = returned.reshape(-1, returned.shape[-1])
    return flat_back[target].reshape(tok_rows, top_count, returned.shape[-1])


def slot_shards(tokens, expert_ids, combine_weights, lift_weights, down_weights, cotangent):
    tok_rows, top_count = expert_ids.shape
    local_experts = lift_weights.shape[0]
    hidden_width = down_weights.shape[1]
    model_width = tokens.shape[1]
    owners = lax.axis_size("expert")
    all_experts = local_experts * owners
    capacity = max(2, 3 * tok_rows * top_count // (2 * all_experts))
    slot_total = tok_rows * top_count
    flat_ids = expert_ids.reshape(-1)
    onehot = (flat_ids[:, None] == jnp.arange(all_experts, dtype=jnp.int32)[None, :]).astype(
        jnp.int32
    )
    ranking = jnp.sum(jnp.cumsum(onehot, axis=0) * onehot, axis=1) - 1
    target = (flat_ids % local_experts * owners + flat_ids // local_experts) * capacity + ranking
    source_of = (
        jnp.full((all_experts * capacity,), -1, jnp.int32)
        .at[target]
        .set(jnp.arange(slot_total, dtype=jnp.int32))
    )
    filled = (source_of >= 0)[:, None]
    source_slot = jnp.maximum(source_of, 0)
    source_row = source_slot // top_count
    slot_gates = combine_weights.reshape(-1)[source_slot]
    buffer_shape = (local_experts, owners, capacity, model_width)
    rows_shape = (local_experts, owners * capacity, model_width)
    send_rows = jnp.where(filled, tokens[source_row], jnp.zeros((), jnp.bfloat16)).reshape(
        buffer_shape
    )
    send_back = jnp.where(
        filled, slot_gates[:, None] * cotangent[source_row].astype(jnp.float32), 0.0
    )
    send_back = send_back.astype(jnp.bfloat16).reshape(buffer_shape)
    recv_rows = lax.all_to_all(
        send_rows, "expert", split_axis=1, concat_axis=1, tiled=True
    ).reshape(rows_shape)
    part_rows = recv_rows
    portion = lax.all_gather(lift_weights, "dp", axis=1, tiled=True)
    gate_term = jnp.einsum(
        "erd,edf->erf", part_rows, portion[:, :, :hidden_width], preferred_element_type=jnp.float32
    )
    up_term = jnp.einsum(
        "erd,edf->erf", part_rows, portion[:, :, hidden_width:], preferred_element_type=jnp.float32
    )
    gate_term, up_term = (gate_term, up_term)
    swished, slopes = swish_parts(gate_term)
    activated = (swished * up_term).astype(jnp.bfloat16)
    portion = lax.all_gather(down_weights, "dp", axis=2, tiled=True)
    result = jnp.stack(
        [
            jnp.dot(activated[expert], portion[expert], preferred_element_type=jnp.float32).astype(
                jnp.bfloat16
            )
            for expert in range(local_experts)
        ]
    )
    returned = lax.all_to_all(
        result.reshape(buffer_shape), "expert", split_axis=1, concat_axis=1, tiled=True
    )
    recv_back = lax.all_to_all(
        send_back, "expert", split_axis=1, concat_axis=1, tiled=True
    ).reshape(rows_shape)
    part_back = recv_back
    act_grad = jnp.einsum(
        "ern,efn->erf",
        part_back,
        lax.all_gather(down_weights, "dp", axis=2, tiled=True),
        preferred_element_type=jnp.float32,
    )
    grad_gate = (act_grad * up_term * slopes).astype(jnp.bfloat16)
    grad_up = (act_grad * swished).astype(jnp.bfloat16)
    portion = lax.all_gather(lift_weights, "dp", axis=1, tiled=True)
    contract = (((1,), (1,)), ((), ()))
    outputs = []
    for expert in range(local_experts):
        first = lax.dot_general(
            grad_gate[expert],
            portion[expert, :, :hidden_width],
            contract,
            preferred_element_type=jnp.float32,
        )
        second = lax.dot_general(
            grad_up[expert],
            portion[expert, :, hidden_width:],
            contract,
            preferred_element_type=jnp.float32,
        )
        outputs.append((first + second).astype(jnp.bfloat16))
    input_grads = jnp.stack(outputs)
    returned_grads = lax.all_to_all(
        input_grads.reshape(buffer_shape), "expert", split_axis=1, concat_axis=1, tiled=True
    )
    picked = collect(returned, target, tok_rows, top_count)
    layer_output = jnp.sum(combine_weights[:, :, None] * picked.astype(jnp.float32), axis=1).astype(
        jnp.bfloat16
    )
    grads_picked = collect(returned_grads, target, tok_rows, top_count)
    token_grads = jnp.sum(grads_picked.astype(jnp.float32), axis=1).astype(jnp.bfloat16)
    part_rows = recv_rows
    part_back = recv_back
    gate_grad = jnp.einsum("ern,erf->nef", part_rows, grad_gate, preferred_element_type=jnp.float32)
    up_grad = jnp.einsum("ern,erf->nef", part_rows, grad_up, preferred_element_type=jnp.float32)
    down_grad = jnp.einsum("ern,erf->nef", part_back, activated, preferred_element_type=jnp.float32)
    summed = lax.psum_scatter(
        jnp.concatenate([gate_grad, up_grad, down_grad], axis=2).astype(jnp.bfloat16),
        "dp",
        scatter_dimension=0,
        tiled=True,
    ).astype(jnp.float32)
    lift_grads = jnp.transpose(summed[:, :, : 2 * hidden_width], (1, 0, 2)).astype(jnp.bfloat16)
    down_grads = jnp.transpose(summed[:, :, 2 * hidden_width :], (1, 2, 0)).astype(jnp.bfloat16)
    return (layer_output, token_grads, lift_grads, down_grads)


def dot(left, right, left_dim, right_dim):
    return lax.dot_general(
        left, right, (((left_dim,), (right_dim,)), ((), ())), preferred_element_type=jnp.float32
    )


def spread(block, owners):
    copies = jnp.broadcast_to(block[None], (owners,) + block.shape)
    return lax.all_to_all(copies, "expert", split_axis=0, concat_axis=0, tiled=True)


def dense_shards(tokens, expert_ids, combine_weights, lift_weights, down_weights, cotangent):
    tok_rows, top_count = expert_ids.shape
    local_experts = lift_weights.shape[0]
    hidden_width = down_weights.shape[1]
    model_width = tokens.shape[1]
    owners = lax.axis_size("expert")
    all_rows = owners * tok_rows
    all_experts = owners * local_experts
    both = jnp.concatenate([lift_weights, jnp.transpose(down_weights, (0, 2, 1))], axis=2)
    both = lax.all_gather(both, "dp", axis=1, tiled=True)
    lift, down = both[:, :, : 2 * hidden_width], both[:, :, 2 * hidden_width :]
    named = expert_ids[:, :, None] == jnp.arange(all_experts, dtype=jnp.int32)[None, None, :]
    dense = jnp.sum(jnp.where(named, combine_weights[:, :, None], 0.0), axis=1)
    sent = jnp.transpose(dense.reshape(tok_rows, owners, local_experts), (1, 2, 0))
    gates = lax.all_to_all(sent, "expert", split_axis=0, concat_axis=0, tiled=True)
    gates = jnp.transpose(gates, (1, 0, 2)).reshape(local_experts, all_rows, 1)
    rows = spread(tokens, owners).reshape(all_rows, model_width)
    back = spread(cotangent, owners).reshape(all_rows, model_width).astype(jnp.float32)
    weighted, grads, parts = [], [], []
    for expert in range(local_experts):
        gate_term = dot(rows, lift[expert, :, :hidden_width], 1, 0)
        up_term = dot(rows, lift[expert, :, hidden_width:], 1, 0)
        back_in = (gates[expert] * back).astype(jnp.bfloat16)
        act_grad = dot(back_in, down[expert], 1, 0)
        swished, slopes = swish_parts(gate_term)
        activated = (swished * up_term).astype(jnp.bfloat16)
        grad_gate = (act_grad * up_term * slopes).astype(jnp.bfloat16)
        grad_up = (act_grad * swished).astype(jnp.bfloat16)
        parts.append(
            jnp.concatenate(
                [dot(rows, grad_gate, 0, 0), dot(rows, grad_up, 0, 0), dot(back_in, activated, 0, 0)],
                axis=1,
            ).astype(jnp.bfloat16)
        )
        weighted.append((gates[expert] * activated.astype(jnp.float32)).astype(jnp.bfloat16))
        grads.append((grad_gate, grad_up))
    summed = lax.psum_scatter(jnp.stack(parts), "dp", scatter_dimension=1, tiled=True)
    lift_grads = summed[:, :, : 2 * hidden_width]
    down_grads = jnp.transpose(summed[:, :, 2 * hidden_width :], (0, 2, 1))

    def returned(total):
        blocks = total.astype(jnp.bfloat16).reshape(owners, tok_rows, model_width)
        pieces = lax.all_to_all(blocks, "expert", split_axis=0, concat_axis=0, tiled=True)
        return jnp.sum(pieces.astype(jnp.float32), axis=0).astype(jnp.bfloat16)

    layer_output = returned(
        sum(dot(weighted[expert], down[expert], 1, 1) for expert in range(local_experts))
    )
    token_grads = returned(
        sum(
            dot(grads[expert][0], lift[expert, :, :hidden_width], 1, 1)
            + dot(grads[expert][1], lift[expert, :, hidden_width:], 1, 1)
            for expert in range(local_experts)
        )
    )
    return (layer_output, token_grads, lift_grads, down_grads)


def shards(tokens, expert_ids, combine_weights, lift_weights, down_weights, cotangent):
    tok_rows, top_count = expert_ids.shape
    local_experts = lift_weights.shape[0]
    all_experts = local_experts * lax.axis_size("expert")
    capacity = max(2, 3 * tok_rows * top_count // (2 * all_experts))
    plan = dense_shards if tok_rows <= local_experts * capacity else slot_shards
    return plan(tokens, expert_ids, combine_weights, lift_weights, down_weights, cotangent)


def solution(mesh):
    in_specs = (
        P(("expert", "dp"), None),
        P(("expert", "dp"), None),
        P(("expert", "dp"), None),
        P("expert", "dp", None),
        P("expert", None, "dp"),
        P(("expert", "dp"), None),
    )
    out_specs = (
        P(("expert", "dp"), None),
        P(("expert", "dp"), None),
        P("expert", "dp", None),
        P("expert", None, "dp"),
    )
    return jax.shard_map(shards, mesh=mesh, in_specs=in_specs, out_specs=out_specs, check_vma=False)
```

```python
import functools

import jax
import jax.numpy as jnp
from jax import lax
from jax.experimental import pallas as pl
from jax.experimental.pallas import tpu as pltpu
from jax.sharding import PartitionSpec as P


def swish_parts(gate_part):
    sigmoid_val = jax.nn.sigmoid(gate_part)
    return (gate_part * sigmoid_val, sigmoid_val * (1.0 + gate_part * (1.0 - sigmoid_val)))


def collect(returned, target, tok_rows, top_count):
    flat_back = returned.reshape(-1, returned.shape[-1])
    return flat_back[target].reshape(tok_rows, top_count, returned.shape[-1])


def slot_shards(tokens, expert_ids, combine_weights, lift_weights, down_weights, cotangent):
    tok_rows, top_count = expert_ids.shape
    local_experts = lift_weights.shape[0]
    hidden_width = down_weights.shape[1]
    model_width = tokens.shape[1]
    owners = lax.axis_size("expert")
    all_experts = local_experts * owners
    capacity = max(2, 3 * tok_rows * top_count // (2 * all_experts))
    slot_total = tok_rows * top_count
    flat_ids = expert_ids.reshape(-1)
    onehot = (flat_ids[:, None] == jnp.arange(all_experts, dtype=jnp.int32)[None, :]).astype(
        jnp.int32
    )
    ranking = jnp.sum(jnp.cumsum(onehot, axis=0) * onehot, axis=1) - 1
    target = (flat_ids % local_experts * owners + flat_ids // local_experts) * capacity + ranking
    source_of = (
        jnp.full((all_experts * capacity,), -1, jnp.int32)
        .at[target]
        .set(jnp.arange(slot_total, dtype=jnp.int32))
    )
    filled = (source_of >= 0)[:, None]
    source_slot = jnp.maximum(source_of, 0)
    source_row = source_slot // top_count
    slot_gates = combine_weights.reshape(-1)[source_slot]
    buffer_shape = (local_experts, owners, capacity, model_width)
    rows_shape = (local_experts, owners * capacity, model_width)
    send_rows = jnp.where(filled, tokens[source_row], jnp.zeros((), jnp.bfloat16)).reshape(
        buffer_shape
    )
    send_back = jnp.where(
        filled, slot_gates[:, None] * cotangent[source_row].astype(jnp.float32), 0.0
    )
    send_back = send_back.astype(jnp.bfloat16).reshape(buffer_shape)
    recv_rows = lax.all_to_all(
        send_rows, "expert", split_axis=1, concat_axis=1, tiled=True
    ).reshape(rows_shape)
    part_rows = recv_rows
    portion = lax.all_gather(lift_weights, "dp", axis=1, tiled=True)
    gate_term = jnp.einsum(
        "erd,edf->erf", part_rows, portion[:, :, :hidden_width], preferred_element_type=jnp.float32
    )
    up_term = jnp.einsum(
        "erd,edf->erf", part_rows, portion[:, :, hidden_width:], preferred_element_type=jnp.float32
    )
    gate_term, up_term = (gate_term, up_term)
    swished, slopes = swish_parts(gate_term)
    activated = (swished * up_term).astype(jnp.bfloat16)
    portion = lax.all_gather(down_weights, "dp", axis=2, tiled=True)
    result = jnp.stack(
        [
            jnp.dot(activated[expert], portion[expert], preferred_element_type=jnp.float32).astype(
                jnp.bfloat16
            )
            for expert in range(local_experts)
        ]
    )
    returned = lax.all_to_all(
        result.reshape(buffer_shape), "expert", split_axis=1, concat_axis=1, tiled=True
    )
    recv_back = lax.all_to_all(
        send_back, "expert", split_axis=1, concat_axis=1, tiled=True
    ).reshape(rows_shape)
    part_back = recv_back
    act_grad = jnp.einsum(
        "ern,efn->erf",
        part_back,
        lax.all_gather(down_weights, "dp", axis=2, tiled=True),
        preferred_element_type=jnp.float32,
    )
    grad_gate = (act_grad * up_term * slopes).astype(jnp.bfloat16)
    grad_up = (act_grad * swished).astype(jnp.bfloat16)
    portion = lax.all_gather(lift_weights, "dp", axis=1, tiled=True)
    contract = (((1,), (1,)), ((), ()))
    outputs = []
    for expert in range(local_experts):
        first = lax.dot_general(
            grad_gate[expert],
            portion[expert, :, :hidden_width],
            contract,
            preferred_element_type=jnp.float32,
        )
        second = lax.dot_general(
            grad_up[expert],
            portion[expert, :, hidden_width:],
            contract,
            preferred_element_type=jnp.float32,
        )
        outputs.append((first + second).astype(jnp.bfloat16))
    input_grads = jnp.stack(outputs)
    returned_grads = lax.all_to_all(
        input_grads.reshape(buffer_shape), "expert", split_axis=1, concat_axis=1, tiled=True
    )
    picked = collect(returned, target, tok_rows, top_count)
    layer_output = jnp.sum(combine_weights[:, :, None] * picked.astype(jnp.float32), axis=1).astype(
        jnp.bfloat16
    )
    grads_picked = collect(returned_grads, target, tok_rows, top_count)
    token_grads = jnp.sum(grads_picked.astype(jnp.float32), axis=1).astype(jnp.bfloat16)
    part_rows = recv_rows
    part_back = recv_back
    gate_grad = jnp.einsum("ern,erf->nef", part_rows, grad_gate, preferred_element_type=jnp.float32)
    up_grad = jnp.einsum("ern,erf->nef", part_rows, grad_up, preferred_element_type=jnp.float32)
    down_grad = jnp.einsum("ern,erf->nef", part_back, activated, preferred_element_type=jnp.float32)
    summed = lax.psum_scatter(
        jnp.concatenate([gate_grad, up_grad, down_grad], axis=2).astype(jnp.bfloat16),
        "dp",
        scatter_dimension=0,
        tiled=True,
    ).astype(jnp.float32)
    lift_grads = jnp.transpose(summed[:, :, : 2 * hidden_width], (1, 0, 2)).astype(jnp.bfloat16)
    down_grads = jnp.transpose(summed[:, :, 2 * hidden_width :], (1, 2, 0)).astype(jnp.bfloat16)
    return (layer_output, token_grads, lift_grads, down_grads)


MESH = pl.DeviceIdType.MESH


def dot(left, right, left_dim, right_dim):
    return lax.dot_general(
        left, right, (((left_dim,), (right_dim,)), ((), ())), preferred_element_type=jnp.float32
    )


def fused(owners, planes, per_expert, *refs):
    (tok_in, cot_in, gate_in, packed, part_out, layer_out, grad_out) = refs[:7]
    (weights, parts, from_left, from_right) = refs[7:11]
    (tok_all, cot_all, gate_all, tok_flip, cot_flip) = refs[11:16]
    (weighted, hidden_grads, totals, paired_in, paired, chip_in) = refs[16:22]
    (own_sem, w_send, w_recv, p_send, p_recv) = refs[22:27]
    (direct_send, direct_recv, pass_send, pass_recv) = refs[27:31]
    (pair_send, pair_recv, chip_send, chip_recv) = refs[31:35]
    stages, slice_rows, packed_width = packed.shape
    width = packed_width // 3
    tok_rows, model_width = tok_in.shape
    hops = planes - 1
    chips = owners // 2
    e, z = lax.axis_index("expert"), lax.axis_index("dp")
    chip, core = e // 2, e % 2
    partner = chip * 2 + 1 - core
    experts = stages // per_expert

    def at(device, plane):
        return (device, plane)

    def chip_at(delta):
        return lax.rem(chip + delta, chips)

    barrier = pltpu.get_barrier_semaphore()
    for delta in range(1, chips):
        pl.semaphore_signal(
            barrier, inc=1, device_id=at(chip_at(delta) * 2 + core, z), device_id_type=MESH
        )
    pl.semaphore_signal(barrier, inc=1, device_id=at(partner, z), device_id_type=MESH)

    @pl.when(z > 0)
    def _():
        pl.semaphore_signal(barrier, inc=1, device_id=at(e, z - 1), device_id_type=MESH)

    @pl.when(z < planes - 1)
    def _():
        pl.semaphore_signal(barrier, inc=1, device_id=at(e, z + 1), device_id_type=MESH)

    end = (z == 0) | (z == planes - 1)

    @pl.when(end)
    def _():
        pl.semaphore_wait(barrier, chips + 1)

    @pl.when(jnp.logical_not(end))
    def _():
        pl.semaphore_wait(barrier, chips + 2)

    def remote(src, dst, send, recv, device):
        return pltpu.make_async_remote_copy(
            src_ref=src, dst_ref=dst, send_sem=send, recv_sem=recv,
            device_id=device, device_id_type=MESH,
        )

    arrays = ((tok_in, tok_all), (cot_in, cot_all), (gate_in, gate_all))

    def own_copies():
        copies = [
            pltpu.make_async_copy(source, full.at[e], own_sem.at[i])
            for i, (source, full) in enumerate(arrays)
        ]
        return copies + [
            pltpu.make_async_copy(packed.at[s], weights.at[s, z], own_sem.at[len(arrays) + s])
            for s in range(stages)
        ]

    def direct(i, delta):
        source, full = arrays[i]
        return remote(
            source, full.at[e], direct_send.at[i, delta], direct_recv.at[i, delta],
            at(chip_at(delta) * 2 + core, z),
        )

    def passed(i, delta):
        source, full = arrays[i]
        origin = chip_at(chips - delta) * 2 + core
        return remote(
            source if delta == 0 else full.at[origin], full.at[e if delta == 0 else origin],
            pass_send.at[i, delta], pass_recv.at[i, delta], at(partner, z),
        )

    kinds = range(len(arrays))
    for copy in own_copies():
        copy.start()
    for i in kinds:
        for delta in range(1, chips):
            direct(i, delta).start()
        passed(i, 0).start()

    def gather(way, hop, s):
        origin = z - hop if way == 0 else z + hop
        source = packed.at[s] if hop == 0 else weights.at[s, origin]
        return remote(
            source, weights.at[s, origin], w_send.at[way, hop], w_recv.at[way, hop, s],
            at(e, z + 1 if way == 0 else z - 1),
        )

    def gather_sends(way, hop):
        if way == 0:
            return (z >= hop) & (z < planes - 1)
        return (z + hop <= planes - 1) & (z > 0)

    def gather_takes(way, hop):
        return z >= hop + 1 if way == 0 else z + hop + 1 <= planes - 1

    def arrived(way, hop, s):
        origin = z - 1 - hop if way == 0 else z + 1 + hop
        landed = weights.at[s, origin]
        return remote(landed, landed, w_send.at[way, hop], w_recv.at[way, hop, s], at(e, z))

    def reduce(way, hop, s):
        if way == 0:
            span, full, device = pl.ds(hop + 1, planes - 1 - hop), from_left, z + 1
        else:
            span, full, device = pl.ds(0, planes - 1 - hop), from_right, z - 1
        return remote(
            parts.at[s, span], full.at[s, span], p_send.at[way], p_recv.at[way, s], at(e, device)
        )

    def reducer(way, hop):
        return hop if way == 0 else planes - 1 - hop

    def compute(s):
        expert = e * experts + s // per_expert

        def forward(i, carry):
            pair = pl.ds(i * 2, 2)
            rows = tok_all[pair].reshape(2 * tok_rows, model_width)
            back = cot_all[pair].reshape(2 * tok_rows, model_width)
            gates = gate_all[pair].reshape(2 * tok_rows, gate_in.shape[1])
            lane = lax.broadcasted_iota(jnp.int32, gates.shape, 1)
            gate = jnp.sum(jnp.where(lane == expert, gates, 0.0), axis=1, keepdims=True)
            whole = weights[s].reshape(model_width, packed_width)
            hidden = dot(rows, whole[:, : 2 * width], 1, 0)
            act_grad = dot(back, whole[:, 2 * width :], 1, 0) * gate
            gate_term, up_term = hidden[:, :width], hidden[:, width:]
            sigmoid_val = 1.0 / (1.0 + jnp.exp(-gate_term))
            swished = gate_term * sigmoid_val
            slopes = sigmoid_val * (1.0 + gate_term * (1.0 - sigmoid_val))
            place = pl.ds(i * 2 * tok_rows, 2 * tok_rows)
            weighted[s, place, :] = (swished * up_term * gate).astype(jnp.bfloat16)
            hidden_grads[s, place, :width] = (act_grad * up_term * slopes).astype(jnp.bfloat16)
            hidden_grads[s, place, width:] = (act_grad * swished).astype(jnp.bfloat16)
            return carry

        lax.fori_loop(0, chips, forward, 0)

        def backward(d, carry):
            parts[s, d, :, : 2 * width] = dot(tok_flip[d], hidden_grads[s], 1, 0).astype(
                jnp.bfloat16
            )
            parts[s, d, :, 2 * width :] = dot(cot_flip[d], weighted[s], 1, 0).astype(jnp.bfloat16)
            return carry

        lax.fori_loop(0, planes, backward, 0)

    def pair_copy(a, q):
        return remote(
            totals.at[a, q * 2 + 1 - core], paired_in.at[a, q],
            pair_send.at[a, q], pair_recv.at[a, q], at(partner, z),
        )

    def chip_copy(a, delta):
        return remote(
            paired.at[a, chip_at(delta)], chip_in.at[a, delta],
            chip_send.at[a, delta], chip_recv.at[a, delta], at(chip_at(delta) * 2 + core, z),
        )

    def finish_rows():
        def rows_of(i, carry):
            place = pl.ds(i * 2 * tok_rows, 2 * tok_rows)
            for o in range(planes):
                columns = slice(o * slice_rows, (o + 1) * slice_rows)
                outs = grads = 0.0
                for s in range(stages):
                    outs += dot(weighted[s, place, :], weights[s, o, :, 2 * width :], 1, 1)
                    grads += dot(hidden_grads[s, place, :], weights[s, o, :, : 2 * width], 1, 1)
                shape = (2, tok_rows, slice_rows)
                totals[0, pl.ds(i * 2, 2), :, columns] = outs.astype(jnp.bfloat16).reshape(shape)
                totals[1, pl.ds(i * 2, 2), :, columns] = grads.astype(jnp.bfloat16).reshape(shape)
            return carry

        lax.fori_loop(0, chips, rows_of, 0)

    def step(k, carry):
        for way in range(2):
            for hop in range(hops):
                s = k - 1 - hop
                live = (s >= 0) & (s < stages)

                @pl.when(live & gather_takes(way, hop))
                def _():
                    arrived(way, hop, s).wait_recv()

                @pl.when(live & gather_sends(way, hop))
                def _():
                    gather(way, hop, s).wait_send()

        for way in range(2):
            for hop in range(hops):
                s = k - 1 - (hops + 1) - hop
                live = (s >= 0) & (s < stages)

                @pl.when(live & (z == reducer(way, hop)))
                def _():
                    reduce(way, hop, s).wait_send()

                @pl.when(live & (z == reducer(way, hop + 1)))
                def _():
                    reduce(way, hop, s).wait_recv()
                    onward = planes - 2 - hop
                    full = from_left if way == 0 else from_right
                    for step_to in range(onward):
                        d = hop + 2 + step_to if way == 0 else step_to
                        parts[s, d] = (
                            parts[s, d].astype(jnp.float32) + full[s, d].astype(jnp.float32)
                        ).astype(jnp.bfloat16)

        for way in range(2):
            for hop in range(hops):
                s = k - hop

                @pl.when((s >= 0) & (s < stages) & gather_sends(way, hop))
                def _():
                    gather(way, hop, s).start()

                t = k - (hops + 1) - hop

                @pl.when((t >= 0) & (t < stages) & (z == reducer(way, hop)))
                def _():
                    reduce(way, hop, t).start()

        @pl.when(k == hops - 1)
        def _():
            for i in kinds:
                for delta in range(1, chips):
                    direct(i, delta).wait_recv()
                    passed(i, delta).start()

        @pl.when(k == hops)
        def _():
            for copy in own_copies():
                copy.wait()
            for i in kinds:
                for delta in range(chips):
                    passed(i, delta).wait()
                for delta in range(1, chips):
                    direct(i, delta).wait_send()

            def flip(j, carry):
                for d in range(planes):
                    columns = slice(d * slice_rows, (d + 1) * slice_rows)
                    for full, flipped in ((tok_all, tok_flip), (cot_all, cot_flip)):
                        block = full[j, :, columns].astype(jnp.float32)
                        flipped[d, :, j * tok_rows : (j + 1) * tok_rows] = block.T.astype(
                            jnp.bfloat16
                        )
                return carry

            for j in range(owners):
                flip(j, 0)

        @pl.when((k >= hops) & (k < hops + stages))
        def _():
            compute(k - hops)

        @pl.when(k == hops + stages)
        def _():
            finish_rows()
            for a in range(2):
                for q in range(chips):
                    pair_copy(a, q).start()

        @pl.when(k == hops + stages + 1)
        def _():
            for a in range(2):
                for q in range(chips):
                    pair_copy(a, q).wait()
                    paired[a, q] = (
                        totals[a, q * 2 + core].astype(jnp.float32)
                        + paired_in[a, q].astype(jnp.float32)
                    ).astype(jnp.bfloat16)
            for a in range(2):
                for delta in range(1, chips):
                    chip_copy(a, delta).start()

        s = k - (2 * hops + 1)

        @pl.when((s >= 0) & (s < stages))
        def _():
            mine = parts[s, z].astype(jnp.float32)

            @pl.when(z == 0)
            def _():
                part_out[s] = (mine + from_right[s, z].astype(jnp.float32)).astype(jnp.bfloat16)

            @pl.when(z == planes - 1)
            def _():
                part_out[s] = (mine + from_left[s, z].astype(jnp.float32)).astype(jnp.bfloat16)

            @pl.when((z > 0) & (z < planes - 1))
            def _():
                sides = from_left[s, z].astype(jnp.float32) + from_right[s, z].astype(jnp.float32)
                part_out[s] = (mine + sides).astype(jnp.bfloat16)

        return carry

    lax.fori_loop(0, stages + 2 * hops + 1, step, 0)
    for a, result in enumerate((layer_out, grad_out)):
        total = paired[a, chip].astype(jnp.float32)
        for delta in range(1, chips):
            chip_copy(a, delta).wait()
            total += chip_in[a, delta].astype(jnp.float32)
        result[...] = total.astype(jnp.bfloat16)


def dense_shards(tokens, expert_ids, combine_weights, lift_weights, down_weights, cotangent):
    tok_rows, top_count = expert_ids.shape
    experts, slice_rows, _ = lift_weights.shape
    hidden_width = down_weights.shape[1]
    model_width = tokens.shape[1]
    owners, planes = lax.axis_size("expert"), lax.axis_size("dp")
    chips = owners // 2
    all_rows = owners * tok_rows
    lanes = -(-owners * experts // 128) * 128
    width = 128 if hidden_width % 128 == 0 else hidden_width
    per_expert = hidden_width // width
    stages = experts * per_expert
    named = expert_ids[:, :, None] == jnp.arange(lanes, dtype=jnp.int32)[None, None, :]
    gates = jnp.sum(jnp.where(named, combine_weights[:, :, None], 0.0), axis=1)
    packed = jnp.concatenate(
        [lift_weights, jnp.transpose(down_weights, (0, 2, 1))], axis=2
    ).reshape(experts, slice_rows, 3, per_expert, width)
    packed = jnp.transpose(packed, (0, 3, 1, 2, 4)).reshape(stages, slice_rows, 3 * width)
    bf16, dma = jnp.bfloat16, pltpu.SemaphoreType.DMA
    full = (stages, planes, slice_rows, 3 * width)
    vmem = pl.BlockSpec(memory_space=pltpu.VMEM)
    parts, layer_output, token_grads = pl.pallas_call(
        functools.partial(fused, owners, planes, per_expert),
        out_shape=(
            jax.ShapeDtypeStruct(packed.shape, bf16),
            jax.ShapeDtypeStruct(tokens.shape, bf16),
            jax.ShapeDtypeStruct(tokens.shape, bf16),
        ),
        in_specs=[vmem] * 4,
        out_specs=[vmem] * 3,
        scratch_shapes=[
            pltpu.VMEM(full, bf16),
            pltpu.VMEM(full, bf16),
            pltpu.VMEM(full, bf16),
            pltpu.VMEM(full, bf16),
            pltpu.VMEM((owners, tok_rows, model_width), bf16),
            pltpu.VMEM((owners, tok_rows, model_width), bf16),
            pltpu.VMEM((owners, tok_rows, lanes), jnp.float32),
            pltpu.VMEM((planes, slice_rows, all_rows), bf16),
            pltpu.VMEM((planes, slice_rows, all_rows), bf16),
            pltpu.VMEM((stages, all_rows, width), bf16),
            pltpu.VMEM((stages, all_rows, 2 * width), bf16),
            pltpu.VMEM((2, owners, tok_rows, model_width), bf16),
            pltpu.VMEM((2, chips, tok_rows, model_width), bf16),
            pltpu.VMEM((2, chips, tok_rows, model_width), bf16),
            pltpu.VMEM((2, chips, tok_rows, model_width), bf16),
            dma((3 + stages,)),
            dma((2, planes)),
            dma((2, planes, stages)),
            dma((2,)),
            dma((2, stages)),
            dma((3, chips)),
            dma((3, chips)),
            dma((3, chips)),
            dma((3, chips)),
            dma((2, chips)),
            dma((2, chips)),
            dma((2, chips)),
            dma((2, chips)),
        ],
        compiler_params=pltpu.CompilerParams(
            collective_id=0, has_side_effects=True, vmem_limit_bytes=60 * 1024 * 1024
        ),
    )(tokens, cotangent, gates, packed)
    parts = parts.reshape(experts, per_expert, slice_rows, 3, width)
    parts = jnp.transpose(parts, (0, 2, 3, 1, 4)).reshape(experts, slice_rows, 3 * hidden_width)
    lift_grads = parts[:, :, : 2 * hidden_width]
    down_grads = jnp.transpose(parts[:, :, 2 * hidden_width :], (0, 2, 1))
    return (layer_output, token_grads, lift_grads, down_grads)


def shards(tokens, expert_ids, combine_weights, lift_weights, down_weights, cotangent):
    tok_rows, top_count = expert_ids.shape
    local_experts = lift_weights.shape[0]
    all_experts = local_experts * lax.axis_size("expert")
    capacity = max(2, 3 * tok_rows * top_count // (2 * all_experts))
    plan = dense_shards if tok_rows <= local_experts * capacity else slot_shards
    return plan(tokens, expert_ids, combine_weights, lift_weights, down_weights, cotangent)


def solution(mesh):
    in_specs = (
        P(("expert", "dp"), None),
        P(("expert", "dp"), None),
        P(("expert", "dp"), None),
        P("expert", "dp", None),
        P("expert", None, "dp"),
        P(("expert", "dp"), None),
    )
    out_specs = (
        P(("expert", "dp"), None),
        P(("expert", "dp"), None),
        P("expert", "dp", None),
        P("expert", None, "dp"),
    )
    return jax.shard_map(shards, mesh=mesh, in_specs=in_specs, out_specs=out_specs, check_vma=False)
```

```python
import functools

import jax
import jax.numpy as jnp
from jax import lax
from jax.experimental import pallas as pl
from jax.experimental.pallas import tpu as pltpu
from jax.sharding import PartitionSpec as P


def swish_parts(gate_part):
    sigmoid_val = jax.nn.sigmoid(gate_part)
    return (gate_part * sigmoid_val, sigmoid_val * (1.0 + gate_part * (1.0 - sigmoid_val)))


def collect(returned, target, tok_rows, top_count):
    flat_back = returned.reshape(-1, returned.shape[-1])
    return flat_back[target].reshape(tok_rows, top_count, returned.shape[-1])


def slot_shards(tokens, expert_ids, combine_weights, lift_weights, down_weights, cotangent):
    tok_rows, top_count = expert_ids.shape
    local_experts = lift_weights.shape[0]
    hidden_width = down_weights.shape[1]
    model_width = tokens.shape[1]
    owners = lax.axis_size("expert")
    all_experts = local_experts * owners
    capacity = max(2, 3 * tok_rows * top_count // (2 * all_experts))
    slot_total = tok_rows * top_count
    flat_ids = expert_ids.reshape(-1)
    onehot = (flat_ids[:, None] == jnp.arange(all_experts, dtype=jnp.int32)[None, :]).astype(
        jnp.int32
    )
    ranking = jnp.sum(jnp.cumsum(onehot, axis=0) * onehot, axis=1) - 1
    target = (flat_ids % local_experts * owners + flat_ids // local_experts) * capacity + ranking
    source_of = (
        jnp.full((all_experts * capacity,), -1, jnp.int32)
        .at[target]
        .set(jnp.arange(slot_total, dtype=jnp.int32))
    )
    filled = (source_of >= 0)[:, None]
    source_slot = jnp.maximum(source_of, 0)
    source_row = source_slot // top_count
    slot_gates = combine_weights.reshape(-1)[source_slot]
    buffer_shape = (local_experts, owners, capacity, model_width)
    rows_shape = (local_experts, owners * capacity, model_width)
    send_rows = jnp.where(filled, tokens[source_row], jnp.zeros((), jnp.bfloat16)).reshape(
        buffer_shape
    )
    send_back = jnp.where(
        filled, slot_gates[:, None] * cotangent[source_row].astype(jnp.float32), 0.0
    )
    send_back = send_back.astype(jnp.bfloat16).reshape(buffer_shape)
    recv_rows = lax.all_to_all(
        send_rows, "expert", split_axis=1, concat_axis=1, tiled=True
    ).reshape(rows_shape)
    part_rows = recv_rows
    portion = lax.all_gather(lift_weights, "dp", axis=1, tiled=True)
    gate_term = jnp.einsum(
        "erd,edf->erf", part_rows, portion[:, :, :hidden_width], preferred_element_type=jnp.float32
    )
    up_term = jnp.einsum(
        "erd,edf->erf", part_rows, portion[:, :, hidden_width:], preferred_element_type=jnp.float32
    )
    gate_term, up_term = (gate_term, up_term)
    swished, slopes = swish_parts(gate_term)
    activated = (swished * up_term).astype(jnp.bfloat16)
    portion = lax.all_gather(down_weights, "dp", axis=2, tiled=True)
    result = jnp.stack(
        [
            jnp.dot(activated[expert], portion[expert], preferred_element_type=jnp.float32).astype(
                jnp.bfloat16
            )
            for expert in range(local_experts)
        ]
    )
    returned = lax.all_to_all(
        result.reshape(buffer_shape), "expert", split_axis=1, concat_axis=1, tiled=True
    )
    recv_back = lax.all_to_all(
        send_back, "expert", split_axis=1, concat_axis=1, tiled=True
    ).reshape(rows_shape)
    part_back = recv_back
    act_grad = jnp.einsum(
        "ern,efn->erf",
        part_back,
        lax.all_gather(down_weights, "dp", axis=2, tiled=True),
        preferred_element_type=jnp.float32,
    )
    grad_gate = (act_grad * up_term * slopes).astype(jnp.bfloat16)
    grad_up = (act_grad * swished).astype(jnp.bfloat16)
    portion = lax.all_gather(lift_weights, "dp", axis=1, tiled=True)
    contract = (((1,), (1,)), ((), ()))
    outputs = []
    for expert in range(local_experts):
        first = lax.dot_general(
            grad_gate[expert],
            portion[expert, :, :hidden_width],
            contract,
            preferred_element_type=jnp.float32,
        )
        second = lax.dot_general(
            grad_up[expert],
            portion[expert, :, hidden_width:],
            contract,
            preferred_element_type=jnp.float32,
        )
        outputs.append((first + second).astype(jnp.bfloat16))
    input_grads = jnp.stack(outputs)
    returned_grads = lax.all_to_all(
        input_grads.reshape(buffer_shape), "expert", split_axis=1, concat_axis=1, tiled=True
    )
    picked = collect(returned, target, tok_rows, top_count)
    layer_output = jnp.sum(combine_weights[:, :, None] * picked.astype(jnp.float32), axis=1).astype(
        jnp.bfloat16
    )
    grads_picked = collect(returned_grads, target, tok_rows, top_count)
    token_grads = jnp.sum(grads_picked.astype(jnp.float32), axis=1).astype(jnp.bfloat16)
    part_rows = recv_rows
    part_back = recv_back
    gate_grad = jnp.einsum("ern,erf->nef", part_rows, grad_gate, preferred_element_type=jnp.float32)
    up_grad = jnp.einsum("ern,erf->nef", part_rows, grad_up, preferred_element_type=jnp.float32)
    down_grad = jnp.einsum("ern,erf->nef", part_back, activated, preferred_element_type=jnp.float32)
    summed = lax.psum_scatter(
        jnp.concatenate([gate_grad, up_grad, down_grad], axis=2).astype(jnp.bfloat16),
        "dp",
        scatter_dimension=0,
        tiled=True,
    ).astype(jnp.float32)
    lift_grads = jnp.transpose(summed[:, :, : 2 * hidden_width], (1, 0, 2)).astype(jnp.bfloat16)
    down_grads = jnp.transpose(summed[:, :, 2 * hidden_width :], (1, 2, 0)).astype(jnp.bfloat16)
    return (layer_output, token_grads, lift_grads, down_grads)


MESH = pl.DeviceIdType.MESH


def dot(left, right, left_dim, right_dim):
    return lax.dot_general(
        left, right, (((left_dim,), (right_dim,)), ((), ())), preferred_element_type=jnp.float32
    )


def fused(owners, planes, per_expert, *refs):
    (tok_in, cot_in, gate_in, packed, lift_out, down_out, layer_out, grad_out) = refs[:8]
    (weights, parts, from_left, from_right) = refs[8:12]
    (tok_all, cot_all, gate_all, tok_flip, cot_flip) = refs[12:17]
    (weighted, hidden_grads, totals, paired_in, paired, chip_in) = refs[17:23]
    (own_sem, w_send, w_recv, p_send, p_recv) = refs[23:28]
    (direct_send, direct_recv, pass_send, pass_recv) = refs[28:32]
    (pair_send, pair_recv, chip_send, chip_recv) = refs[32:36]
    stages, slice_rows, packed_width = packed.shape
    width = packed_width // 3
    tok_rows, model_width = tok_in.shape
    hops = planes - 1
    chips = owners // 2
    e, z = lax.axis_index("expert"), lax.axis_index("dp")
    chip, core = e // 2, e % 2
    partner = chip * 2 + 1 - core
    experts = stages // per_expert

    def at(device, plane):
        return (device, plane)

    def chip_at(delta):
        return lax.rem(chip + delta, chips)

    barrier = pltpu.get_barrier_semaphore()
    for delta in range(1, chips):
        pl.semaphore_signal(
            barrier, inc=1, device_id=at(chip_at(delta) * 2 + core, z), device_id_type=MESH
        )
    pl.semaphore_signal(barrier, inc=1, device_id=at(partner, z), device_id_type=MESH)

    @pl.when(z > 0)
    def _():
        pl.semaphore_signal(barrier, inc=1, device_id=at(e, z - 1), device_id_type=MESH)

    @pl.when(z < planes - 1)
    def _():
        pl.semaphore_signal(barrier, inc=1, device_id=at(e, z + 1), device_id_type=MESH)

    end = (z == 0) | (z == planes - 1)

    @pl.when(end)
    def _():
        pl.semaphore_wait(barrier, chips + 1)

    @pl.when(jnp.logical_not(end))
    def _():
        pl.semaphore_wait(barrier, chips + 2)

    def remote(src, dst, send, recv, device):
        return pltpu.make_async_remote_copy(
            src_ref=src, dst_ref=dst, send_sem=send, recv_sem=recv,
            device_id=device, device_id_type=MESH,
        )

    arrays = ((tok_in, tok_all), (cot_in, cot_all), (gate_in, gate_all))

    def own_copies():
        copies = [
            pltpu.make_async_copy(source, full.at[e], own_sem.at[i])
            for i, (source, full) in enumerate(arrays)
        ]
        return copies + [
            pltpu.make_async_copy(packed.at[s], weights.at[s, z], own_sem.at[len(arrays) + s])
            for s in range(stages)
        ]

    def direct(i, delta):
        source, full = arrays[i]
        return remote(
            source, full.at[e], direct_send.at[i, delta], direct_recv.at[i, delta],
            at(chip_at(delta) * 2 + core, z),
        )

    def passed(i, delta):
        source, full = arrays[i]
        origin = chip_at(chips - delta) * 2 + core
        return remote(
            source if delta == 0 else full.at[origin], full.at[e if delta == 0 else origin],
            pass_send.at[i, delta], pass_recv.at[i, delta], at(partner, z),
        )

    kinds = range(len(arrays))
    for copy in own_copies():
        copy.start()
    for i in kinds:
        for delta in range(1, chips):
            direct(i, delta).start()
        passed(i, 0).start()

    def gather(way, hop, s):
        origin = z - hop if way == 0 else z + hop
        source = packed.at[s] if hop == 0 else weights.at[s, origin]
        return remote(
            source, weights.at[s, origin], w_send.at[way, hop, s], w_recv.at[way, hop, s],
            at(e, z + 1 if way == 0 else z - 1),
        )

    def gather_sends(way, hop):
        if way == 0:
            return (z >= hop) & (z < planes - 1)
        return (z + hop <= planes - 1) & (z > 0)

    def gather_takes(way, hop):
        return z >= hop + 1 if way == 0 else z + hop + 1 <= planes - 1

    def arrived(way, hop, s):
        origin = z - 1 - hop if way == 0 else z + 1 + hop
        landed = weights.at[s, origin]
        return remote(landed, landed, w_send.at[way, hop, s], w_recv.at[way, hop, s], at(e, z))

    def reduce(way, hop, s):
        if way == 0:
            span, full, device = pl.ds(hop + 1, planes - 1 - hop), from_left, z + 1
        else:
            span, full, device = pl.ds(0, planes - 1 - hop), from_right, z - 1
        return remote(
            parts.at[s, span], full.at[s, span], p_send.at[way, s], p_recv.at[way, s], at(e, device)
        )

    def reducer(way, hop):
        return hop if way == 0 else planes - 1 - hop

    def compute(s):
        expert = e * experts + s // per_expert

        def forward(i, carry):
            pair = pl.ds(i * 2, 2)
            rows = tok_all[pair].reshape(2 * tok_rows, model_width)
            back = cot_all[pair].reshape(2 * tok_rows, model_width)
            gates = gate_all[pair].reshape(2 * tok_rows, gate_in.shape[1])
            lane = lax.broadcasted_iota(jnp.int32, gates.shape, 1)
            gate = jnp.sum(jnp.where(lane == expert, gates, 0.0), axis=1, keepdims=True)
            whole = weights[s].reshape(model_width, packed_width)
            hidden = dot(rows, whole[:, : 2 * width], 1, 0)
            act_grad = dot(back, whole[:, 2 * width :], 1, 0) * gate
            gate_term, up_term = hidden[:, :width], hidden[:, width:]
            sigmoid_val = 1.0 / (1.0 + jnp.exp(-gate_term))
            swished = gate_term * sigmoid_val
            slopes = sigmoid_val * (1.0 + gate_term * (1.0 - sigmoid_val))
            place = pl.ds(i * 2 * tok_rows, 2 * tok_rows)
            weighted[s, place, :] = (swished * up_term * gate).astype(jnp.bfloat16)
            hidden_grads[s, place, :width] = (act_grad * up_term * slopes).astype(jnp.bfloat16)
            hidden_grads[s, place, width:] = (act_grad * swished).astype(jnp.bfloat16)
            return carry

        lax.fori_loop(0, chips, forward, 0)

        def backward(d, carry):
            parts[s, d, :, : 2 * width] = dot(tok_flip[d], hidden_grads[s], 1, 0).astype(
                jnp.bfloat16
            )
            parts[s, d, :, 2 * width :] = dot(cot_flip[d], weighted[s], 1, 0).astype(jnp.bfloat16)
            return carry

        lax.fori_loop(0, planes, backward, 0)

    def pair_copy(a, q):
        return remote(
            totals.at[a, q * 2 + 1 - core], paired_in.at[a, q],
            pair_send.at[a, q], pair_recv.at[a, q], at(partner, z),
        )

    def chip_copy(a, delta):
        return remote(
            paired.at[a, chip_at(delta)], chip_in.at[a, delta],
            chip_send.at[a, delta], chip_recv.at[a, delta], at(chip_at(delta) * 2 + core, z),
        )

    def finish_rows():
        def rows_of(i, carry):
            place = pl.ds(i * 2 * tok_rows, 2 * tok_rows)
            for o in range(planes):
                columns = slice(o * slice_rows, (o + 1) * slice_rows)
                outs = grads = 0.0
                for s in range(stages):
                    outs += dot(weighted[s, place, :], weights[s, o, :, 2 * width :], 1, 1)
                    grads += dot(hidden_grads[s, place, :], weights[s, o, :, : 2 * width], 1, 1)
                shape = (2, tok_rows, slice_rows)
                totals[0, pl.ds(i * 2, 2), :, columns] = outs.astype(jnp.bfloat16).reshape(shape)
                totals[1, pl.ds(i * 2, 2), :, columns] = grads.astype(jnp.bfloat16).reshape(shape)
            return carry

        lax.fori_loop(0, chips, rows_of, 0)

    def step(k, carry):
        for way in range(2):
            for hop in range(hops):
                s = k - 1 - hop
                live = (s >= 0) & (s < stages)

                @pl.when(live & gather_takes(way, hop))
                def _():
                    arrived(way, hop, s).wait_recv()

                @pl.when(live & gather_sends(way, hop))
                def _():
                    gather(way, hop, s).wait_send()

        for way in range(2):
            for hop in range(hops - 1, -1, -1):
                s = k - hop if hop else k + 1

                @pl.when((s >= 0) & (s < stages) & gather_sends(way, hop))
                def _():
                    gather(way, hop, s).start()

        for way in range(2):
            for hop in range(hops):
                s = k - 1 - (hops + 1) - hop
                live = (s >= 0) & (s < stages)

                @pl.when(live & (z == reducer(way, hop)))
                def _():
                    reduce(way, hop, s).wait_send()

                @pl.when(live & (z == reducer(way, hop + 1)))
                def _():
                    reduce(way, hop, s).wait_recv()
                    onward = planes - 2 - hop
                    full = from_left if way == 0 else from_right
                    for step_to in range(onward):
                        d = hop + 2 + step_to if way == 0 else step_to
                        parts[s, d] = (
                            parts[s, d].astype(jnp.float32) + full[s, d].astype(jnp.float32)
                        ).astype(jnp.bfloat16)

        for way in range(2):
            for hop in range(1, hops):
                t = k - (hops + 1) - hop

                @pl.when((t >= 0) & (t < stages) & (z == reducer(way, hop)))
                def _():
                    reduce(way, hop, t).start()

        @pl.when(k == hops - 1)
        def _():
            for i in kinds:
                for delta in range(1, chips):
                    direct(i, delta).wait_recv()
                    passed(i, delta).start()

        @pl.when(k == hops)
        def _():
            for copy in own_copies():
                copy.wait()
            for i in kinds:
                for delta in range(chips):
                    passed(i, delta).wait()
                for delta in range(1, chips):
                    direct(i, delta).wait_send()

            def flip(j, carry):
                for d in range(planes):
                    columns = slice(d * slice_rows, (d + 1) * slice_rows)
                    for full, flipped in ((tok_all, tok_flip), (cot_all, cot_flip)):
                        block = full[j, :, columns].astype(jnp.float32)
                        flipped[d, :, j * tok_rows : (j + 1) * tok_rows] = block.T.astype(
                            jnp.bfloat16
                        )
                return carry

            for j in range(owners):
                flip(j, 0)

        @pl.when(k == hops + stages)
        def _():
            for a in range(2):
                for q in range(chips):
                    pair_copy(a, q).wait()
                    paired[a, q] = (
                        totals[a, q * 2 + core].astype(jnp.float32)
                        + paired_in[a, q].astype(jnp.float32)
                    ).astype(jnp.bfloat16)
            for a in range(2):
                for delta in range(1, chips):
                    chip_copy(a, delta).start()

        @pl.when((k >= hops) & (k < hops + stages))
        def _():
            compute(k - hops)
            for way in range(2):

                @pl.when(z == reducer(way, 0))
                def _():
                    reduce(way, 0, k - hops).start()

        @pl.when(k == hops + stages - 1)
        def _():
            finish_rows()
            for a in range(2):
                for q in range(chips):
                    pair_copy(a, q).start()

        s = k - (2 * hops + 1)

        @pl.when((s >= 0) & (s < stages))
        def _():
            mine = parts[s, z].astype(jnp.float32)

            def store(total):
                owned, chunk = lax.div(s, per_expert), lax.rem(s, per_expert)
                gate_at = pl.multiple_of(chunk * width, width)
                up_at = pl.multiple_of((chunk + per_expert) * width, width)
                lift_out[owned, :, pl.ds(gate_at, width)] = total[:, :width].astype(jnp.bfloat16)
                lift_out[owned, :, pl.ds(up_at, width)] = total[:, width : 2 * width].astype(
                    jnp.bfloat16
                )
                down_out[owned, pl.ds(gate_at, width), :] = total[:, 2 * width :].T.astype(
                    jnp.bfloat16
                )

            @pl.when(z == 0)
            def _():
                store(mine + from_right[s, z].astype(jnp.float32))

            @pl.when(z == planes - 1)
            def _():
                store(mine + from_left[s, z].astype(jnp.float32))

            @pl.when((z > 0) & (z < planes - 1))
            def _():
                sides = from_left[s, z].astype(jnp.float32) + from_right[s, z].astype(jnp.float32)
                store(mine + sides)

        return carry

    for way in range(2):

        @pl.when(gather_sends(way, 0))
        def _():
            gather(way, 0, 0).start()

    lax.fori_loop(0, stages + 2 * hops + 1, step, 0)
    for a, result in enumerate((layer_out, grad_out)):
        total = paired[a, chip].astype(jnp.float32)
        for delta in range(1, chips):
            chip_copy(a, delta).wait()
            total += chip_in[a, delta].astype(jnp.float32)
        result[...] = total.astype(jnp.bfloat16)


def dense_shards(tokens, expert_ids, combine_weights, lift_weights, down_weights, cotangent):
    tok_rows, top_count = expert_ids.shape
    experts, slice_rows, _ = lift_weights.shape
    hidden_width = down_weights.shape[1]
    model_width = tokens.shape[1]
    owners, planes = lax.axis_size("expert"), lax.axis_size("dp")
    chips = owners // 2
    all_rows = owners * tok_rows
    lanes = -(-owners * experts // 128) * 128
    width = 128 if hidden_width % 128 == 0 else hidden_width
    per_expert = hidden_width // width
    stages = experts * per_expert
    named = expert_ids[:, :, None] == jnp.arange(lanes, dtype=jnp.int32)[None, None, :]
    gates = jnp.sum(jnp.where(named, combine_weights[:, :, None], 0.0), axis=1)
    packed = jnp.concatenate(
        [lift_weights, jnp.transpose(down_weights, (0, 2, 1))], axis=2
    ).reshape(experts, slice_rows, 3, per_expert, width)
    packed = jnp.transpose(packed, (0, 3, 1, 2, 4)).reshape(stages, slice_rows, 3 * width)
    bf16, dma = jnp.bfloat16, pltpu.SemaphoreType.DMA
    full = (stages, planes, slice_rows, 3 * width)
    vmem = pl.BlockSpec(memory_space=pltpu.VMEM)
    lift_grads, down_grads, layer_output, token_grads = pl.pallas_call(
        functools.partial(fused, owners, planes, per_expert),
        out_shape=(
            jax.ShapeDtypeStruct(lift_weights.shape, bf16),
            jax.ShapeDtypeStruct(down_weights.shape, bf16),
            jax.ShapeDtypeStruct(tokens.shape, bf16),
            jax.ShapeDtypeStruct(tokens.shape, bf16),
        ),
        in_specs=[vmem] * 4,
        out_specs=[vmem] * 4,
        scratch_shapes=[
            pltpu.VMEM(full, bf16),
            pltpu.VMEM(full, bf16),
            pltpu.VMEM(full, bf16),
            pltpu.VMEM(full, bf16),
            pltpu.VMEM((owners, tok_rows, model_width), bf16),
            pltpu.VMEM((owners, tok_rows, model_width), bf16),
            pltpu.VMEM((owners, tok_rows, lanes), jnp.float32),
            pltpu.VMEM((planes, slice_rows, all_rows), bf16),
            pltpu.VMEM((planes, slice_rows, all_rows), bf16),
            pltpu.VMEM((stages, all_rows, width), bf16),
            pltpu.VMEM((stages, all_rows, 2 * width), bf16),
            pltpu.VMEM((2, owners, tok_rows, model_width), bf16),
            pltpu.VMEM((2, chips, tok_rows, model_width), bf16),
            pltpu.VMEM((2, chips, tok_rows, model_width), bf16),
            pltpu.VMEM((2, chips, tok_rows, model_width), bf16),
            dma((3 + stages,)),
            dma((2, planes, stages)),
            dma((2, planes, stages)),
            dma((2, stages)),
            dma((2, stages)),
            dma((3, chips)),
            dma((3, chips)),
            dma((3, chips)),
            dma((3, chips)),
            dma((2, chips)),
            dma((2, chips)),
            dma((2, chips)),
            dma((2, chips)),
        ],
        compiler_params=pltpu.CompilerParams(
            collective_id=0, has_side_effects=True, vmem_limit_bytes=60 * 1024 * 1024
        ),
    )(tokens, cotangent, gates, packed)
    return (layer_output, token_grads, lift_grads, down_grads)


def shards(tokens, expert_ids, combine_weights, lift_weights, down_weights, cotangent):
    tok_rows, top_count = expert_ids.shape
    local_experts = lift_weights.shape[0]
    all_experts = local_experts * lax.axis_size("expert")
    capacity = max(2, 3 * tok_rows * top_count // (2 * all_experts))
    plan = dense_shards if tok_rows <= local_experts * capacity else slot_shards
    return plan(tokens, expert_ids, combine_weights, lift_weights, down_weights, cotangent)


def solution(mesh):
    in_specs = (
        P(("expert", "dp"), None),
        P(("expert", "dp"), None),
        P(("expert", "dp"), None),
        P("expert", "dp", None),
        P("expert", None, "dp"),
        P(("expert", "dp"), None),
    )
    out_specs = (
        P(("expert", "dp"), None),
        P(("expert", "dp"), None),
        P("expert", "dp", None),
        P("expert", None, "dp"),
    )
    return jax.shard_map(shards, mesh=mesh, in_specs=in_specs, out_specs=out_specs, check_vma=False)
```
